512 devices in a mesh: seq: 16 (over z), head: 32 (over x, y, core).
Axes of the slice: x: 4, y: 4, z: 16, core: 2. Of those that a mesh axis runs over, the one named last changes fastest.
Arguments:
- queries: bfloat16 [16384, 8192], P('seq', 'head'), may hold values from -6 to 6
- keys: bfloat16 [16384, 8192], P('seq', 'head'), may hold values from -1 to 1
- values: bfloat16 [16384, 8192], P('seq', 'head'), may hold values from -40 to 40
- log_decay: float32 [64, 16384], P('head', 'seq'), may hold values from -1 to 0
- gain: float32 [8192], P('head'), may hold values from 0.25 to 1.75
- out_grad: bfloat16 [16384, 8192], P('seq', 'head'), may hold values from -16 to 16
Outputs:
- output: bfloat16 [16384, 8192], P('seq', 'head')
- query_grad: bfloat16 [16384, 8192], P('seq', 'head')
- key_grad: bfloat16 [16384, 8192], P('seq', 'head')
- value_grad: bfloat16 [16384, 8192], P('seq', 'head')
- gain_grad: float32 [8192], P('head')
The draws below stay inside these ranges and needn't reach their ends.
All inputs are finite; a program needn't handle non-finite values.
Results may differ from the reference program's by a relative error of at most 0.001.
Values sent between devices are 32-bit elements; how exact they have to be, the bound alone decides.
No kernel may reach another device: no remote copies, remote signals or barrier semaphores. Data moves between devices by JAX's collectives and lax.ppermute only.
A program may use at most 64 MiB of HBM per device.

```python
import math
import jax
import jax.numpy as jnp
from jax import lax

HEAD_TOTAL = 64
HEAD_DIM = 128
TOK_DEV = 1024
LENGTH = 16384


def head_rates(key):
    rate_key = jax.random.fold_in(key, 7001)
    pick_key, fast_key, slow_key = jax.random.split(rate_key, 3)
    fast_share = 0.5
    is_fast = jax.random.uniform(pick_key, (HEAD_TOTAL,)) < fast_share
    fast_low = math.log(max(1.0 / 50.0, 3.0 / TOK_DEV))
    fast_high = math.log(max(1.0 / 30.0, 4.0 / TOK_DEV))
    fast = jnp.exp(jax.random.uniform(fast_key, (HEAD_TOTAL,), minval=fast_low, maxval=fast_high))
    slow = jnp.exp(jax.random.uniform(slow_key, (HEAD_TOTAL,), minval=math.log(0.05 / LENGTH), maxval=math.log(0.6 / LENGTH)))
    return jnp.where(is_fast, fast, slow)


def draw_log_decay(key, part):
    rates = head_rates(key)
    spike_seed_key = jax.random.fold_in(key, 7002)
    position_seed_key, layer_depth_key = jax.random.split(spike_seed_key)
    token_places = jax.random.randint(position_seed_key, (HEAD_TOTAL, 2), 0, LENGTH)
    spike_log_values = jnp.log(jax.random.uniform(layer_depth_key, (HEAD_TOTAL, 2), minval=0.5, maxval=0.8))
    token_positions = jnp.arange(LENGTH)[None, :]
    first_operand = jnp.where(token_positions == token_places[:, 0:1], spike_log_values[:, 0:1], 0.0)
    second_operand = jnp.where(token_positions == token_places[:, 1:2], spike_log_values[:, 1:2], 0.0)
    return (jnp.minimum(first_operand, second_operand) - rates[:, None]).astype(jnp.float32)


def draw_keys(key, part):
    rates = head_rates(key)
    scale = jnp.minimum(1.0, jnp.sqrt(40.0 * rates)) / math.sqrt(HEAD_DIM)
    base_key = jax.random.fold_in(key, 7003)
    base = jnp.clip(jax.random.normal(base_key, (LENGTH, HEAD_TOTAL, HEAD_DIM)), -3.0, 3.0)
    return (base * scale[None, :, None]).reshape(LENGTH, HEAD_TOTAL * HEAD_DIM).astype(jnp.bfloat16)


def draw_values(key, part):
    jitter_key, row_key, base_key = jax.random.split(jax.random.fold_in(key, 7004), 3)
    head_scale = 10.0 ** (jnp.arange(HEAD_TOTAL, dtype=jnp.float32) / (HEAD_TOTAL - 1))
    head_scale = head_scale * jnp.exp(jax.random.uniform(jitter_key, (HEAD_TOTAL,), minval=math.log(0.8), maxval=math.log(1.25)))
    base = jnp.clip(jax.random.normal(base_key, (LENGTH, HEAD_TOTAL, HEAD_DIM)), -3.0, 3.0)
    row_scale = jnp.exp(jax.random.uniform(row_key, (LENGTH,), minval=0.0, maxval=math.log(10.0)))
    result = base * head_scale[None, :, None] * row_scale[:, None, None] / 10.0
    return result.reshape(LENGTH, HEAD_TOTAL * HEAD_DIM).astype(jnp.bfloat16)


def draw_out_grad(key, part):
    base_key = jax.random.fold_in(jax.random.fold_in(key, 7005), 0)
    jitter_key = jax.random.fold_in(jax.random.fold_in(key, 7005), 2)
    along = jnp.arange(LENGTH, dtype=jnp.float32) / (LENGTH - 1)
    jitter = jnp.exp(jax.random.uniform(jitter_key, (LENGTH,), minval=math.log(0.7), maxval=math.log(1.4)))
    base = jnp.clip(jax.random.normal(base_key, (LENGTH, HEAD_TOTAL * HEAD_DIM)), -3.0, 3.0)
    rising = 0.5 * 3.0 ** along
    return (base * (rising * jitter)[:, None]).astype(jnp.bfloat16)


def block_scale(own_key, dims, cuts, low, largest):
    loudness, own = 1.0, jax.random.fold_in(own_key, 6)
    for dim, shards_of in cuts:
        heights = jnp.exp(jax.random.uniform(jax.random.fold_in(own, dim), (shards_of,), jnp.float32, low / len(cuts), largest / len(cuts)))
        loudness = loudness * jnp.repeat(heights, dims[dim] // shards_of).reshape([-1 if axis == dim else 1 for axis in range(len(dims))])
    return loudness


def scatter_about(stream_key, shape, width, most, shards=(), kind=jnp.bfloat16):
    values = width * jax.random.normal(stream_key, shape, jnp.float32)
    if shards:
        values = values * block_scale(stream_key, shape, shards, -0.22, 0.18)
    return jnp.clip(values, -most, most).astype(kind)


def setup_inputs(seed: int = 0) -> dict:
    arg_keys = jax.random.split(jax.random.key(seed), 7)
    queries = scatter_about(arg_keys[0], (LENGTH, HEAD_TOTAL * HEAD_DIM), 1.0, 6.0, ((0, 16), (1, 32)))
    keys = draw_keys(jax.random.fold_in(arg_keys[6], 71), 0)
    values = draw_values(jax.random.fold_in(arg_keys[6], 71), 0)
    log_decay = draw_log_decay(jax.random.fold_in(arg_keys[6], 71), 0)
    gain = jnp.clip(1.0 + 0.15 * jax.random.normal(arg_keys[4], (HEAD_TOTAL * HEAD_DIM,), jnp.float32), 0.25, 1.75)
    out_grad = draw_out_grad(jax.random.fold_in(arg_keys[6], 71), 0)
    return {"queries": queries, "keys": keys, "values": values, "log_decay": log_decay, "gain": gain, "out_grad": out_grad}


epsilon = 1e-06
highest = lax.Precision.HIGHEST

def attention(query_heads, key_heads, value_heads, log_decay):
    head_count, length, head_width = query_heads.shape
    block_rows = min(256, length)
    block_count = length // block_rows

    def blocks(matrix):
        return matrix.reshape(head_count, block_count, block_rows, head_width).transpose(1, 0, 2, 3)
    decay_blocks = log_decay.reshape(head_count, block_count, block_rows).transpose(1, 0, 2)
    causal = jnp.arange(block_rows)[:, None] >= jnp.arange(block_rows)[None, :]

    def block_step(carry_state, inputs):
        query_block, key_block, value_block, decay_block = inputs
        decay_sum = jnp.cumsum(decay_block, axis=1)
        block_total = decay_sum[:, -1]
        mask_decay = jnp.exp(jnp.where(causal, decay_sum[:, :, None] - decay_sum[:, None, :], -1e+30))
        scores = jnp.einsum('hid,hjd->hij', query_block, key_block, precision=highest) * mask_decay
        inside = jnp.einsum('hij,hjd->hid', scores, value_block, precision=highest)
        carried = jnp.exp(decay_sum)[:, :, None] * jnp.einsum('hid,hde->hie', query_block, carry_state, precision=highest)
        weighted = key_block * jnp.exp(block_total[:, None] - decay_sum)[:, :, None]
        carry_state = jnp.exp(block_total)[:, None, None] * carry_state + jnp.einsum('hjd,hje->hde', weighted, value_block, precision=highest)
        return (carry_state, inside + carried)
    initial = jnp.zeros((head_count, head_width, head_width), jnp.float32)
    _, result = lax.scan(jax.checkpoint(block_step), initial, (blocks(query_heads), blocks(key_heads), blocks(value_heads), decay_blocks))
    return result.transpose(1, 0, 2, 3).reshape(head_count, length, head_width)

def reference(queries, keys, values, log_decay, gain, out_grad):
    length, channels = queries.shape

    def to_heads(matrix):
        return matrix.astype(jnp.float32).reshape(length, HEAD_TOTAL, HEAD_DIM).transpose(1, 0, 2)

    def from_heads(heads_array):
        return heads_array.transpose(1, 0, 2).reshape(length, channels).astype(jnp.bfloat16)

    def forward(query_heads, key_heads, value_heads, gain_vector):
        attended = attention(query_heads, key_heads, value_heads, log_decay)
        flattened = attended.transpose(1, 0, 2).reshape(length, channels)
        root_mean = jnp.sqrt(lax.optimization_barrier(jnp.mean(flattened * flattened, axis=1, keepdims=True)) + epsilon)
        return flattened / root_mean * gain_vector
    output, pullback = jax.vjp(forward, to_heads(queries), to_heads(keys), to_heads(values), gain)
    query_grad, key_grad, value_grad, gain_grad = pullback(out_grad.astype(jnp.float32))
    return (output.astype(jnp.bfloat16), from_heads(query_grad), from_heads(key_grad), from_heads(value_grad), gain_grad)
```

```python
import jax
import jax.numpy as jnp
from jax import lax
from jax.experimental import pallas as pl
from jax.experimental.pallas import tpu as pltpu
from jax.sharding import PartitionSpec as P

epsilon = 1e-06
width = 128
block_rows = 256
f32 = jnp.float32
bf16 = jnp.bfloat16


def dot(a, b, a_dim, b_dim):
    return lax.dot_general(a, b, (((a_dim,), (b_dim,)), ((), ())), preferred_element_type=f32)


def split(x):
    high = x.astype(bf16)
    return high, (x - high.astype(f32)).astype(bf16)


def side_by_side(x):
    return jnp.concatenate(split(x), axis=1)


def folded(x):
    return x[:, :width] + x[:, width:]


def dot_split_right(a, b, a_dim, b_dim):
    high, low = split(b)
    return dot(a, high, a_dim, b_dim) + dot(a, low, a_dim, b_dim)


def dot_split_left(a, b, a_dim, b_dim):
    high, low = split(a)
    return dot(high, b, a_dim, b_dim) + dot(low, b, a_dim, b_dim)


def dot_split_both(a, b, a_dim, b_dim):
    a_high, a_low = split(a)
    b_high, b_low = split(b)
    return (
        dot(a_high, b_high, a_dim, b_dim)
        + dot(a_high, b_low, a_dim, b_dim)
        + dot(a_low, b_high, a_dim, b_dim)
    )


def head_columns(ref, head):
    return ref[:, head * width : (head + 1) * width]


def block_of(array, block):
    return array[block * block_rows : (block + 1) * block_rows]


def start_column(table, block):
    return table[:, block : block + 1]


def end_column(table, block, blocks):
    return table[:, blocks + block : blocks + block + 1]


def inner_column(table, block, blocks):
    return table[:, 2 * blocks + block : 2 * blocks + block + 1]


def state_kernel(decay_ref, keys_ref, values_ref, pieces_ref, table_ref, rows_ref):
    heads, tokens = decay_ref.shape
    blocks = tokens // block_rows
    decay = decay_ref[...]
    stacked = jnp.concatenate(
        [
            decay[h : h + 1, b * block_rows : (b + 1) * block_rows]
            for h in range(heads)
            for b in range(blocks)
        ],
        axis=0,
    )
    row = lax.broadcasted_iota(jnp.int32, (block_rows, block_rows), 0)
    column = lax.broadcasted_iota(jnp.int32, (block_rows, block_rows), 1)
    upper = jnp.where(row <= column, 1.0, 0.0).astype(f32)
    sums = jnp.dot(stacked, upper, precision=lax.Precision.HIGHEST, preferred_element_type=f32)
    for h in range(heads):
        inside = sums[h * blocks : (h + 1) * blocks]
        offset = jnp.zeros((1, 1), f32)
        offsets = []
        for b in range(blocks):
            offsets.append(offset)
            offset = offset + inside[b : b + 1, block_rows - 1 : block_rows]
        from_device = inside + jnp.concatenate(offsets, axis=0)
        table = jnp.concatenate(
            [
                jnp.exp(from_device),
                jnp.exp(offset - from_device),
                inside,
                jnp.zeros((width - 3 * blocks, block_rows), f32),
            ],
            axis=0,
        ).T
        table_ref[h] = table
        rows_ref[h] = jnp.concatenate([inside, jnp.zeros((8 - blocks, block_rows), f32)], axis=0)
        values = head_columns(values_ref, h).astype(f32)
        weighted = jnp.concatenate(
            [
                side_by_side(end_column(table, b, blocks) * block_of(values, b))
                for b in range(blocks)
            ],
            axis=0,
        )
        state = folded(dot(head_columns(keys_ref, h), weighted, 0, 0))
        total = jnp.broadcast_to(jnp.exp(offset), (1, width))
        store_pieces(pieces_ref, h, heads, state, total)


def store_pieces(pieces_ref, head, heads, state, extra):
    count = heads * width // slice_rows(pieces_ref.shape[0], heads, extra.shape[0])
    rows = heads * width // count
    stride = rows + extra.shape[0]
    per_head = count // heads
    for index in range(per_head):
        base = (head * per_head + index) * stride
        pieces_ref[base : base + rows] = state[index * rows : (index + 1) * rows]
        pieces_ref[base + rows : base + stride] = extra


def slice_rows(total, heads, extra_rows):
    return heads * width * extra_rows // (total - heads * width)


def decay_mask(table, rows, block, blocks, causal):
    return jnp.exp(
        jnp.where(causal, inner_column(table, block, blocks) - rows[block : block + 1], -1e30)
    )


def causal_mask():
    row = lax.broadcasted_iota(jnp.int32, (block_rows, block_rows), 0)
    column = lax.broadcasted_iota(jnp.int32, (block_rows, block_rows), 1)
    return row >= column


def inside_kernel(queries_ref, keys_ref, values_ref, table_ref, rows_ref, local_ref):
    blocks = queries_ref.shape[0] // block_rows
    causal = causal_mask()
    table = table_ref[0]
    rows = rows_ref[0]
    running = None
    for b in range(blocks):
        part = slice(b * block_rows, (b + 1) * block_rows)
        query, key, value = queries_ref[part], keys_ref[part], values_ref[part]
        mask = decay_mask(table, rows, b, blocks, causal)
        inner = inner_column(table, b, blocks)
        total = inner[block_rows - 1 : block_rows]
        scores = dot(query, key, 1, 1) * mask
        result = dot_split_left(scores, value, 1, 0)
        if b:
            result = result + jnp.exp(inner) * folded(dot(query, side_by_side(running), 1, 0))
        local_ref[part] = result
        if b + 1 < blocks:
            weighted = jnp.exp(total - inner) * value.astype(f32)
            state = folded(dot(key, side_by_side(weighted), 0, 0))
            running = state if b == 0 else jnp.exp(total) * running + state


def prefix_kernel(pieces_ref, entering_ref, *, count):
    rows = entering_ref.shape[0] // count
    stride = pieces_ref.shape[0] // count
    prefix = jnp.zeros((rows, width), f32)
    for index in range(count):
        entering_ref[index * rows : (index + 1) * rows] = prefix
        base = index * stride
        if index + 1 < count:
            prefix = (
                pieces_ref[base + rows : base + rows + 1] * prefix
                + pieces_ref[base : base + rows]
            )


def suffix_kernel(decay_pieces_ref, pieces_ref, leaving_ref, gain_ref, *, count):
    rows = leaving_ref.shape[0] // count
    stride = pieces_ref.shape[0] // count
    decay_stride = decay_pieces_ref.shape[0] // count
    suffix = jnp.zeros((rows, width), f32)
    gain_sum = jnp.zeros(gain_ref.shape, f32)
    for index in reversed(range(count)):
        leaving_ref[index * rows : (index + 1) * rows] = suffix
        base = index * stride
        decay_row = index * decay_stride + rows
        suffix = (
            decay_pieces_ref[decay_row : decay_row + 1] * suffix + pieces_ref[base : base + rows]
        )
        gain_sum = gain_sum + pieces_ref[base + rows : base + stride]
    gain_ref[...] = gain_sum


def attend_kernel(
    queries_ref, grads_ref, gain_ref, local_ref, entering_ref, table_ref, attended_ref, sums_ref
):
    tokens, channels = queries_ref.shape
    heads = channels // width
    blocks = tokens // block_rows
    groups = tokens // width
    lane = lax.broadcasted_iota(jnp.int32, (width, width), 1)
    states = [side_by_side(entering_ref[h * width : (h + 1) * width]) for h in range(heads)]
    gathered = jnp.zeros((width, width), f32)
    for b in range(blocks):
        part = slice(b * block_rows, (b + 1) * block_rows)
        squares = jnp.zeros((block_rows, width), f32)
        products = jnp.zeros((block_rows, width), f32)
        for h in range(heads):
            cut = slice(h * width, (h + 1) * width)
            carried = folded(dot(queries_ref[part, cut], states[h], 1, 0))
            attended = local_ref[part, cut] + start_column(table_ref[h], b) * carried
            attended_ref[part, cut] = attended
            squares = squares + attended * attended
            products = products + grads_ref[part, cut].astype(f32) * gain_ref[:, cut] * attended
        square_sum = jnp.sum(squares, axis=1, keepdims=True)
        product_sum = jnp.sum(products, axis=1, keepdims=True)
        for piece in range(block_rows // width):
            group = b * (block_rows // width) + piece
            inner = slice(piece * width, (piece + 1) * width)
            gathered = jnp.where(lane == group, square_sum[inner], gathered)
            gathered = jnp.where(lane == groups + group, product_sum[inner], gathered)
    compact = gathered.T[: 2 * groups]
    for index in range(sums_ref.shape[0]):
        sums_ref[index] = compact


def grad_kernel(
    sums_ref, attended_ref, grads_ref, gain_ref, queries_ref, table_ref,
    output_ref, attended_grad_ref, pieces_ref, *, total_channels
):
    tokens, channels = queries_ref.shape
    heads = channels // width
    blocks = tokens // block_rows
    groups = tokens // width
    sums = sums_ref[0]
    for index in range(1, sums_ref.shape[0]):
        sums = sums + sums_ref[index]
    inverse = 1.0 / jnp.sqrt(sums[:groups] / total_channels + epsilon)
    mean = inverse * sums[groups:] / total_channels
    scales = jnp.concatenate(
        [inverse, mean, jnp.zeros((width - 2 * groups, width), f32)], axis=0
    ).T
    gain_rows = []
    backs = []
    for h in range(heads):
        cut = slice(h * width, (h + 1) * width)
        gain = gain_ref[:, cut]
        gain_sum = jnp.zeros((1, width), f32)
        weighted = []
        for group in range(groups):
            part = slice(group * width, (group + 1) * width)
            b = group * width // block_rows
            within = (group * width) % block_rows
            inverse_column = scales[:, group : group + 1]
            mean_column = scales[:, groups + group : groups + group + 1]
            grad = grads_ref[part, cut].astype(f32)
            normed = attended_ref[part, cut] * inverse_column
            output_ref[part, cut] = (normed * gain).astype(bf16)
            gain_sum = gain_sum + jnp.sum(grad * normed, axis=0, keepdims=True)
            attended_grad = (grad * gain - normed * mean_column) * inverse_column
            attended_grad_ref[part, cut] = attended_grad
            start = start_column(table_ref[h, within : within + width], b)
            weighted.append(side_by_side(start * attended_grad))
        gain_rows.append(gain_sum)
        backs.append(folded(dot(queries_ref[:, cut], jnp.concatenate(weighted, axis=0), 0, 0)))
    extra = jnp.concatenate(gain_rows, axis=0)
    for h in range(heads):
        store_pieces(pieces_ref, h, heads, backs[h], extra)


def local_grad_kernel(
    queries_ref, keys_ref, values_ref, attended_grad_ref, entering_ref, table_ref, rows_ref,
    query_grad_ref, key_part_ref, value_part_ref
):
    blocks = queries_ref.shape[0] // block_rows
    causal = causal_mask()
    table = table_ref[0]
    rows = rows_ref[0]
    entering = entering_ref[...]
    leaving = None
    for b in range(blocks):
        part = slice(b * block_rows, (b + 1) * block_rows)
        key, value = keys_ref[part], values_ref[part]
        grad_high, grad_low = split(attended_grad_ref[part])
        inner = inner_column(table, b, blocks)
        total = inner[block_rows - 1 : block_rows]
        mask = decay_mask(table, rows, b, blocks, causal)
        score_grad = (dot(grad_high, value, 1, 1) + dot(grad_low, value, 1, 1)) * mask
        state_high, state_low = split(entering)
        carried = (
            dot(grad_high, state_high, 1, 1)
            + dot(grad_high, state_low, 1, 1)
            + dot(grad_low, state_high, 1, 1)
        )
        score_high, score_low = split(score_grad)
        query_grad = dot(score_high, key, 1, 0) + dot(score_low, key, 1, 0)
        query_grad_ref[part] = (query_grad + jnp.exp(inner) * carried).astype(bf16)
        query = queries_ref[part]
        key_part_ref[part] = dot(score_high, query, 0, 0) + dot(score_low, query, 0, 0)
        scores = dot(query, key, 1, 1) * mask
        weights_high, weights_low = split(scores)
        value_part_ref[part] = (
            dot(weights_high, grad_high, 0, 0)
            + dot(weights_high, grad_low, 0, 0)
            + dot(weights_low, grad_high, 0, 0)
        )
        if b + 1 < blocks:
            weighted = jnp.exp(total - inner) * value.astype(f32)
            entering = jnp.exp(total) * entering + folded(dot(key, side_by_side(weighted), 0, 0))
    for b in reversed(range(blocks)):
        part = slice(b * block_rows, (b + 1) * block_rows)
        inner = inner_column(table, b, blocks)
        total = inner[block_rows - 1 : block_rows]
        to_end = jnp.exp(total - inner)
        if b + 1 < blocks:
            leave_high, leave_low = split(leaving)
            value = values_ref[part]
            key = keys_ref[part]
            key_part_ref[part] += to_end * (
                dot(value, leave_high, 1, 1) + dot(value, leave_low, 1, 1)
            )
            value_part_ref[part] += to_end * (
                dot(key, leave_high, 1, 0) + dot(key, leave_low, 1, 0)
            )
        if b:
            weighted = side_by_side(jnp.exp(inner) * attended_grad_ref[part])
            back = folded(dot(queries_ref[part], weighted, 0, 0))
            leaving = back if leaving is None else back + jnp.exp(total) * leaving


def finish_kernel(
    keys_ref, values_ref, leaving_ref, table_ref, key_part_ref, value_part_ref,
    key_grad_ref, value_grad_ref
):
    tokens, channels = keys_ref.shape
    heads = channels // width
    blocks = tokens // block_rows
    for h in range(heads):
        cut = slice(h * width, (h + 1) * width)
        high, low = split(leaving_ref[cut])
        across = jnp.concatenate([high, low], axis=1)
        down = jnp.concatenate([high, low], axis=0)
        for b in range(blocks):
            part = slice(b * block_rows, (b + 1) * block_rows)
            to_end = end_column(table_ref[h], b, blocks)
            key_carry = folded(dot(values_ref[part, cut], down, 1, 1))
            value_carry = folded(dot(keys_ref[part, cut], across, 1, 0))
            key_grad_ref[part, cut] = (key_part_ref[part, cut] + to_end * key_carry).astype(bf16)
            value_grad_ref[part, cut] = (
                value_part_ref[part, cut] + to_end * value_carry
            ).astype(bf16)


def shape(dims, dtype=f32):
    return jax.ShapeDtypeStruct(dims, dtype)


def exchange(pieces, count):
    flat = pieces.reshape(count, 1, pieces.shape[0] // count * width)
    return lax.all_to_all(flat, "seq", 0, 0, tiled=True).reshape(pieces.shape)


def local(queries, keys, values, log_decay, gain, out_grad):
    tokens, channels = queries.shape
    heads = log_decay.shape[0]
    seq_count = lax.axis_size("seq")
    head_count = lax.axis_size("head")
    total_channels = channels * head_count
    state_rows = heads * width
    gain_row = gain.reshape(1, channels)
    groups = tokens // width
    whole = pl.BlockSpec((tokens, width), lambda h: (0, h))
    table_spec = pl.BlockSpec((1, block_rows, width), lambda h: (h, 0, 0))
    rows_spec = pl.BlockSpec((1, 8, block_rows), lambda h: (h, 0, 0))
    state_spec = pl.BlockSpec((width, width), lambda h: (h, 0))

    pieces, table, rows = pl.pallas_call(
        state_kernel,
        out_shape=(
            shape((state_rows + seq_count, width)),
            shape((heads, block_rows, width)),
            shape((heads, 8, block_rows)),
        ),
        name="own_state",
    )(log_decay, keys, values)
    with jax.named_scope("scan_out"):
        arrived = exchange(pieces, seq_count)
    inside = pl.pallas_call(
        inside_kernel,
        out_shape=shape((tokens, channels)),
        grid=(heads,),
        in_specs=[whole, whole, whole, table_spec, rows_spec],
        out_specs=whole,
        cost_estimate=pl.CostEstimate(
            flops=2 * 4 * tokens * block_rows * channels, transcendentals=tokens * block_rows * heads,
            bytes_accessed=5 * tokens * channels * 2,
        ),
        name="inside",
    )(queries, keys, values, table, rows)
    prefixes = pl.pallas_call(
        lambda *refs: prefix_kernel(*refs, count=seq_count),
        out_shape=shape((state_rows, width)),
        name="prefix",
    )(arrived)
    with jax.named_scope("scan_back"):
        entering = exchange(prefixes, seq_count)
    attended, sums = pl.pallas_call(
        attend_kernel,
        out_shape=(shape((tokens, channels)), shape((head_count, 2 * groups, width))),
        name="attend",
    )(queries, out_grad, gain_row, inside, entering, table)
    with jax.named_scope("head_sums"):
        sums = lax.all_to_all(sums, "head", 0, 0, tiled=True)
    output, attended_grad, back_pieces = pl.pallas_call(
        lambda *refs: grad_kernel(*refs, total_channels=float(total_channels)),
        out_shape=(
            shape((tokens, channels), bf16),
            shape((tokens, channels)),
            shape((state_rows + heads * seq_count, width)),
        ),
        name="norm_grad",
    )(sums, attended, out_grad, gain_row, queries, table)
    with jax.named_scope("back_out"):
        back_arrived = exchange(back_pieces, seq_count)
    query_grad, key_part, value_part = pl.pallas_call(
        local_grad_kernel,
        out_shape=(
            shape((tokens, channels), bf16),
            shape((tokens, channels)),
            shape((tokens, channels)),
        ),
        grid=(heads,),
        in_specs=[whole, whole, whole, whole, state_spec, table_spec, rows_spec],
        out_specs=(whole, whole, whole),
        cost_estimate=pl.CostEstimate(
            flops=2 * 14 * tokens * block_rows * channels, transcendentals=tokens * block_rows * heads,
            bytes_accessed=14 * tokens * channels * 2,
        ),
        name="local_grad",
    )(queries, keys, values, attended_grad, entering, table, rows)
    suffixes, gain_sum = pl.pallas_call(
        lambda *refs: suffix_kernel(*refs, count=seq_count),
        out_shape=(shape((state_rows, width)), shape((heads, width))),
        name="suffix",
    )(arrived, back_arrived)
    with jax.named_scope("back_back"):
        leaving = exchange(suffixes, seq_count)
    key_grad, value_grad = pl.pallas_call(
        finish_kernel,
        out_shape=(shape((tokens, channels), bf16), shape((tokens, channels), bf16)),
        name="finish",
    )(keys, values, leaving, table, key_part, value_part)
    return output, query_grad, key_grad, value_grad, gain_sum.reshape(channels)


def solution(mesh):
    in_specs = (
        P("seq", "head"),
        P("seq", "head"),
        P("seq", "head"),
        P("head", "seq"),
        P("head"),
        P("seq", "head"),
    )
    out_specs = (P("seq", "head"), P("seq", "head"), P("seq", "head"), P("seq", "head"), P("head"))
    return jax.shard_map(local, mesh=mesh, in_specs=in_specs, out_specs=out_specs, check_vma=False)
```

```python
import jax
import jax.numpy as jnp
from jax import lax
from jax.experimental import pallas as pl
from jax.experimental.pallas import tpu as pltpu
from jax.sharding import PartitionSpec as P

epsilon = 1e-06
width = 128
block_rows = 256
f32 = jnp.float32
bf16 = jnp.bfloat16


def dot(a, b, a_dim, b_dim):
    return lax.dot_general(a, b, (((a_dim,), (b_dim,)), ((), ())), preferred_element_type=f32)


def split(x):
    high = x.astype(bf16)
    return high, (x - high.astype(f32)).astype(bf16)


def side_by_side(x):
    return jnp.concatenate(split(x), axis=1)


def folded(x):
    return x[:, :width] + x[:, width:]


def dot_split_right(a, b, a_dim, b_dim):
    high, low = split(b)
    return dot(a, high, a_dim, b_dim) + dot(a, low, a_dim, b_dim)


def dot_split_left(a, b, a_dim, b_dim):
    high, low = split(a)
    return dot(high, b, a_dim, b_dim) + dot(low, b, a_dim, b_dim)


def dot_split_both(a, b, a_dim, b_dim):
    a_high, a_low = split(a)
    b_high, b_low = split(b)
    return (
        dot(a_high, b_high, a_dim, b_dim)
        + dot(a_high, b_low, a_dim, b_dim)
        + dot(a_low, b_high, a_dim, b_dim)
    )


def head_columns(ref, head):
    return ref[:, head * width : (head + 1) * width]


def block_of(array, block):
    return array[block * block_rows : (block + 1) * block_rows]


def table_column(table, kind, head, block, blocks):
    index = (3 * head + kind) * blocks + block
    return table[:, index : index + 1]


def start_column(table, head, block, blocks):
    return table_column(table, 0, head, block, blocks)


def end_column(table, head, block, blocks):
    return table_column(table, 1, head, block, blocks)


def inner_column(table, head, block, blocks):
    return table_column(table, 2, head, block, blocks)


def state_kernel(
    decay_ref, far_keys_ref, far_values_ref, pieces_ref, table_ref, rows_ref,
    keys_ref, values_ref, arrivals
):
    heads, tokens = decay_ref.shape
    values_in = pltpu.make_async_copy(far_values_ref, values_ref, arrivals.at[0])
    keys_in = pltpu.make_async_copy(far_keys_ref, keys_ref, arrivals.at[1])
    values_in.start()
    keys_in.start()
    blocks = tokens // block_rows
    decay = decay_ref[...]
    stacked = jnp.concatenate(
        [
            decay[h : h + 1, b * block_rows : (b + 1) * block_rows]
            for h in range(heads)
            for b in range(blocks)
        ],
        axis=0,
    )
    row = lax.broadcasted_iota(jnp.int32, (block_rows, block_rows), 0)
    column = lax.broadcasted_iota(jnp.int32, (block_rows, block_rows), 1)
    upper = jnp.where(row <= column, 1.0, 0.0).astype(f32)
    sums = jnp.dot(stacked, upper, precision=lax.Precision.HIGHEST, preferred_element_type=f32)
    table_rows = []
    totals = []
    for h in range(heads):
        inside = sums[h * blocks : (h + 1) * blocks]
        offset = jnp.zeros((1, 1), f32)
        offsets = []
        for b in range(blocks):
            offsets.append(offset)
            offset = offset + inside[b : b + 1, block_rows - 1 : block_rows]
        from_device = inside + jnp.concatenate(offsets, axis=0)
        table_rows += [jnp.exp(from_device), jnp.exp(offset - from_device), inside]
        totals.append(jnp.broadcast_to(jnp.exp(offset), (1, width)))
    table_rows.append(jnp.zeros((width - 3 * blocks * heads, block_rows), f32))
    table = jnp.concatenate(table_rows, axis=0).T
    table_ref[...] = table
    rows_ref[...] = sums
    values_in.wait()
    keys_in.wait()
    for h in range(heads):
        values = head_columns(values_ref, h).astype(f32)
        weighted = jnp.concatenate(
            [
                side_by_side(end_column(table, h, b, blocks) * block_of(values, b))
                for b in range(blocks)
            ],
            axis=0,
        )
        state = folded(dot(head_columns(keys_ref, h), weighted, 0, 0))
        store_pieces(pieces_ref, h, heads, state, totals[h])


def store_pieces(pieces_ref, head, heads, state, extra):
    count = heads * width // slice_rows(pieces_ref.shape[0], heads, extra.shape[0])
    rows = heads * width // count
    stride = rows + extra.shape[0]
    per_head = count // heads
    for index in range(per_head):
        base = (head * per_head + index) * stride
        pieces_ref[base : base + rows] = state[index * rows : (index + 1) * rows]
        pieces_ref[base + rows : base + stride] = extra


def slice_rows(total, heads, extra_rows):
    return heads * width * extra_rows // (total - heads * width)


def decay_mask(table, rows, head, block, blocks, causal):
    index = head * blocks + block
    inner = inner_column(table, head, block, blocks)
    return jnp.exp(jnp.where(causal, inner - rows[index : index + 1], -1e30))


def causal_mask():
    row = lax.broadcasted_iota(jnp.int32, (block_rows, block_rows), 0)
    column = lax.broadcasted_iota(jnp.int32, (block_rows, block_rows), 1)
    return row >= column


def inside_kernel(
    queries_ref, keys_ref, values_ref, table_ref, rows_ref, gain_in_ref,
    local_ref, gain_ref, order_ref
):
    tokens, channels = queries_ref.shape
    blocks = tokens // block_rows
    causal = causal_mask()
    table = table_ref[...]
    rows = rows_ref[...]
    for h in range(channels // width):
        cut = slice(h * width, (h + 1) * width)
        running = None
        for b in range(blocks):
            part = slice(b * block_rows, (b + 1) * block_rows)
            query, key, value = queries_ref[part, cut], keys_ref[part, cut], values_ref[part, cut]
            mask = decay_mask(table, rows, h, b, blocks, causal)
            inner = inner_column(table, h, b, blocks)
            total = inner[block_rows - 1 : block_rows]
            scores = dot(query, key, 1, 1) * mask
            result = dot_split_left(scores, value, 1, 0)
            if b:
                result = result + jnp.exp(inner) * folded(dot(query, side_by_side(running), 1, 0))
            local_ref[part, cut] = result
            if b + 1 < blocks:
                weighted = jnp.exp(total - inner) * value.astype(f32)
                state = folded(dot(key, side_by_side(weighted), 0, 0))
                running = state if b == 0 else jnp.exp(total) * running + state
    order_ref[...] = jnp.zeros(order_ref.shape, f32)
    gain_ref[...] = gain_in_ref[...]


def prefix_kernel(pieces_ref, order_ref, entering_ref, *, count):
    rows = entering_ref.shape[0] // count
    stride = pieces_ref.shape[0] // count
    prefix = jnp.zeros((rows, width), f32)
    for index in range(count):
        entering_ref[index * rows : (index + 1) * rows] = prefix
        base = index * stride
        if index + 1 < count:
            prefix = (
                pieces_ref[base + rows : base + rows + 1] * prefix
                + pieces_ref[base : base + rows]
            )


def suffix_kernel(
    decay_pieces_ref, pieces_ref, order_ref, leaving_ref, gain_ref, *, count
):
    rows = leaving_ref.shape[0] // count
    stride = pieces_ref.shape[0] // count
    decay_stride = decay_pieces_ref.shape[0] // count
    suffix = jnp.zeros((rows, width), f32)
    gain_sum = jnp.zeros(gain_ref.shape, f32)
    for index in reversed(range(count)):
        leaving_ref[index * rows : (index + 1) * rows] = suffix
        base = index * stride
        decay_row = index * decay_stride + rows
        suffix = (
            decay_pieces_ref[decay_row : decay_row + 1] * suffix + pieces_ref[base : base + rows]
        )
        gain_sum = gain_sum + pieces_ref[base + rows : base + stride]
    gain_ref[...] = gain_sum


def attend_kernel(
    queries_ref, grads_ref, gain_ref, local_ref, entering_ref, table_ref, attended_ref, sums_ref
):
    tokens, channels = queries_ref.shape
    heads = channels // width
    blocks = tokens // block_rows
    groups = tokens // width
    lane = lax.broadcasted_iota(jnp.int32, (width, width), 1)
    states = [side_by_side(entering_ref[h * width : (h + 1) * width]) for h in range(heads)]
    gathered = jnp.zeros((width, width), f32)
    for b in range(blocks):
        part = slice(b * block_rows, (b + 1) * block_rows)
        squares = jnp.zeros((block_rows, width), f32)
        products = jnp.zeros((block_rows, width), f32)
        for h in range(heads):
            cut = slice(h * width, (h + 1) * width)
            carried = folded(dot(queries_ref[part, cut], states[h], 1, 0))
            attended = local_ref[part, cut] + start_column(table_ref, h, b, blocks) * carried
            attended_ref[part, cut] = attended
            squares = squares + attended * attended
            products = products + grads_ref[part, cut].astype(f32) * gain_ref[:, cut] * attended
        square_sum = jnp.sum(squares, axis=1, keepdims=True)
        product_sum = jnp.sum(products, axis=1, keepdims=True)
        for piece in range(block_rows // width):
            group = b * (block_rows // width) + piece
            inner = slice(piece * width, (piece + 1) * width)
            gathered = jnp.where(lane == group, square_sum[inner], gathered)
            gathered = jnp.where(lane == groups + group, product_sum[inner], gathered)
    compact = gathered.T[: 2 * groups]
    for index in range(sums_ref.shape[0]):
        sums_ref[index] = compact


def grad_kernel(
    sums_ref, attended_ref, grads_ref, gain_ref, queries_ref, table_ref,
    far_grad_ref, far_scales_ref, pieces_ref, attended_grad_ref, scales_ref, departures,
    *, total_channels
):
    tokens, channels = queries_ref.shape
    heads = channels // width
    blocks = tokens // block_rows
    groups = tokens // width
    sums = sums_ref[0]
    for index in range(1, sums_ref.shape[0]):
        sums = sums + sums_ref[index]
    inverse = 1.0 / jnp.sqrt(sums[:groups] / total_channels + epsilon)
    mean = inverse * sums[groups:] / total_channels
    scales = jnp.concatenate(
        [inverse, mean, jnp.zeros((width - 2 * groups, width), f32)], axis=0
    ).T
    scales_ref[...] = scales
    leaving = [pltpu.make_async_copy(scales_ref, far_scales_ref, departures.at[heads])]
    leaving[0].start()
    gain_rows = []
    backs = []
    for h in range(heads):
        cut = slice(h * width, (h + 1) * width)
        gain = gain_ref[:, cut]
        gain_sum = jnp.zeros((1, width), f32)
        weighted = []
        for group in range(groups):
            part = slice(group * width, (group + 1) * width)
            b = group * width // block_rows
            within = (group * width) % block_rows
            inverse_column = scales[:, group : group + 1]
            mean_column = scales[:, groups + group : groups + group + 1]
            grad = grads_ref[part, cut].astype(f32)
            normed = attended_ref[part, cut] * inverse_column
            gain_sum = gain_sum + jnp.sum(grad * normed, axis=0, keepdims=True)
            attended_grad = (grad * gain - normed * mean_column) * inverse_column
            attended_grad_ref[part, cut] = attended_grad
            start = start_column(table_ref[within : within + width], h, b, blocks)
            weighted.append(side_by_side(start * attended_grad))
        out = pltpu.make_async_copy(
            attended_grad_ref.at[:, cut], far_grad_ref.at[:, cut], departures.at[h]
        )
        out.start()
        leaving.append(out)
        gain_rows.append(gain_sum)
        backs.append(folded(dot(queries_ref[:, cut], jnp.concatenate(weighted, axis=0), 0, 0)))
    extra = jnp.concatenate(gain_rows, axis=0)
    for h in range(heads):
        store_pieces(pieces_ref, h, heads, backs[h], extra)
    for out in leaving:
        out.wait()


def local_grad_kernel(
    attended_ref, gain_ref, scales_ref, queries_ref, keys_ref, values_ref, attended_grad_ref,
    entering_ref, table_ref, rows_ref,
    output_ref, query_grad_ref, key_part_ref, value_part_ref, order_ref
):
    tokens, channels = keys_ref.shape
    blocks = tokens // block_rows
    causal = causal_mask()
    table = table_ref[...]
    rows = rows_ref[...]
    for h in range(channels // width):
        cut = slice(h * width, (h + 1) * width)
        gain = gain_ref[:, cut]
        for group in range(tokens // width):
            part = slice(group * width, (group + 1) * width)
            normed = attended_ref[part, cut] * scales_ref[:, group : group + 1]
            output_ref[part, cut] = (normed * gain).astype(bf16)
        leaving = [None] * blocks
        for b in reversed(range(1, blocks)):
            part = slice(b * block_rows, (b + 1) * block_rows)
            inner = inner_column(table, h, b, blocks)
            total = inner[block_rows - 1 : block_rows]
            weighted = side_by_side(jnp.exp(inner) * attended_grad_ref[part, cut])
            back = folded(dot(queries_ref[part, cut], weighted, 0, 0))
            if leaving[b] is not None:
                back = back + jnp.exp(total) * leaving[b]
            leaving[b - 1] = back
        entering = entering_ref[cut]
        for b in range(blocks):
            part = slice(b * block_rows, (b + 1) * block_rows)
            query, key, value = queries_ref[part, cut], keys_ref[part, cut], values_ref[part, cut]
            grad_high, grad_low = split(attended_grad_ref[part, cut])
            inner = inner_column(table, h, b, blocks)
            total = inner[block_rows - 1 : block_rows]
            to_end = jnp.exp(total - inner)
            mask = decay_mask(table, rows, h, b, blocks, causal)
            score_grad = (dot(grad_high, value, 1, 1) + dot(grad_low, value, 1, 1)) * mask
            state_high, state_low = split(entering)
            carried = (
                dot(grad_high, state_high, 1, 1)
                + dot(grad_high, state_low, 1, 1)
                + dot(grad_low, state_high, 1, 1)
            )
            score_high, score_low = split(score_grad)
            query_grad = dot(score_high, key, 1, 0) + dot(score_low, key, 1, 0)
            query_grad_ref[part, cut] = (query_grad + jnp.exp(inner) * carried).astype(bf16)
            key_part = dot(score_high, query, 0, 0) + dot(score_low, query, 0, 0)
            weights_high, weights_low = split(dot(query, key, 1, 1) * mask)
            value_part = (
                dot(weights_high, grad_high, 0, 0)
                + dot(weights_high, grad_low, 0, 0)
                + dot(weights_low, grad_high, 0, 0)
            )
            if b + 1 < blocks:
                leave_high, leave_low = split(leaving[b])
                key_part = key_part + to_end * (
                    dot(value, leave_high, 1, 1) + dot(value, leave_low, 1, 1)
                )
                value_part = value_part + to_end * (
                    dot(key, leave_high, 1, 0) + dot(key, leave_low, 1, 0)
                )
                state = folded(dot(key, side_by_side(to_end * value.astype(f32)), 0, 0))
                entering = jnp.exp(total) * entering + state
            key_part_ref[part, cut] = key_part
            value_part_ref[part, cut] = value_part
    order_ref[...] = jnp.zeros(order_ref.shape, f32)


def finish_kernel(
    keys_ref, values_ref, leaving_ref, table_ref, key_part_ref, far_value_part_ref,
    far_key_grad_ref, far_value_grad_ref,
    value_part_ref, key_grad_ref, value_grad_ref, arrivals, departures
):
    tokens, channels = keys_ref.shape
    heads = channels // width
    blocks = tokens // block_rows
    parts = [slice(b * block_rows, (b + 1) * block_rows) for b in range(blocks)]
    arriving = []
    for b, part in enumerate(parts):
        copy = pltpu.make_async_copy(
            far_value_part_ref.at[part], value_part_ref.at[part], arrivals.at[b]
        )
        copy.start()
        arriving.append(copy)
    leaving = []

    def send(near_ref, far_ref, part):
        copy = pltpu.make_async_copy(
            near_ref.at[part], far_ref.at[part], departures.at[len(leaving)]
        )
        copy.start()
        leaving.append(copy)

    states = [split(leaving_ref[h * width : (h + 1) * width]) for h in range(heads)]
    for b, part in enumerate(parts):
        for h in range(heads):
            cut = slice(h * width, (h + 1) * width)
            down = jnp.concatenate(states[h], axis=0)
            carry = folded(dot(values_ref[part, cut], down, 1, 1))
            to_end = end_column(table_ref, h, b, blocks)
            key_grad_ref[part, cut] = (key_part_ref[part, cut] + to_end * carry).astype(bf16)
        send(key_grad_ref, far_key_grad_ref, part)
    for b, part in enumerate(parts):
        arriving[b].wait()
        for h in range(heads):
            cut = slice(h * width, (h + 1) * width)
            across = jnp.concatenate(states[h], axis=1)
            carry = folded(dot(keys_ref[part, cut], across, 1, 0))
            to_end = end_column(table_ref, h, b, blocks)
            value_grad_ref[part, cut] = (
                value_part_ref[part, cut] + to_end * carry
            ).astype(bf16)
        send(value_grad_ref, far_value_grad_ref, part)
    for copy in leaving:
        copy.wait()


def shape(dims, dtype=f32):
    return jax.ShapeDtypeStruct(dims, dtype)


def near(dims, dtype=f32):
    return pltpu.VMEM(dims, dtype)


class Held:
    def __init__(self, array):
        self.array = pltpu.with_memory_space_constraint(array, pltpu.VMEM)


def exchange(pieces, count):
    flat = pieces.reshape(count, 1, pieces.shape[0] // count * width)
    return lax.all_to_all(flat, "seq", 0, 0, tiled=True).reshape(pieces.shape)


class Far:
    def __init__(self, array):
        if isinstance(array, jax.ShapeDtypeStruct):
            self.array = pltpu.HBM(array.shape, array.dtype)
        else:
            self.array = pltpu.with_memory_space_constraint(array, pltpu.HBM)


def spec_of(item):
    if isinstance(item, Far):
        return pl.BlockSpec(memory_space=pltpu.HBM)
    if isinstance(item, Held):
        return pl.BlockSpec(memory_space=pltpu.VMEM)
    return pl.BlockSpec()


def bare(item):
    return item.array if isinstance(item, (Held, Far)) else item


def call(kernel, name, out_shape, operands, flops=0, scratch=()):
    return pl.pallas_call(
        kernel,
        out_shape=tuple(bare(x) for x in out_shape),
        in_specs=[spec_of(x) for x in operands],
        out_specs=tuple(spec_of(x) for x in out_shape),
        scratch_shapes=scratch,
        compiler_params=pltpu.CompilerParams(vmem_limit_bytes=24 * 2**20),
        cost_estimate=pl.CostEstimate(flops=flops, transcendentals=0, bytes_accessed=2**20),
        name=name,
    )(*(bare(x) for x in operands))


def local(queries, keys, values, log_decay, gain, out_grad):
    tokens, channels = queries.shape
    heads = log_decay.shape[0]
    seq_count = lax.axis_size("seq")
    head_count = lax.axis_size("head")
    total_channels = float(channels * head_count)
    state_rows = heads * width
    groups = tokens // width
    tile = (8, width)
    unit = 2 * tokens * block_rows * channels
    token_shape = (tokens, channels)

    pieces, table, rows = call(
        state_kernel, "own_state",
        (
            shape((state_rows + seq_count, width)),
            near((block_rows, width)),
            shape((heads * tokens // block_rows, block_rows)),
        ),
        (log_decay, Far(keys), Far(values)),
        scratch=(
            pltpu.VMEM(token_shape, bf16),
            pltpu.VMEM(token_shape, bf16),
            pltpu.SemaphoreType.DMA((2,)),
        ),
    )
    table = Held(table)
    with jax.named_scope("scan_out"):
        arrived = exchange(pieces, seq_count)
    inside, gain_row, order = call(
        inside_kernel, "inside", (near(token_shape), near((1, channels)), shape(tile)),
        (queries, keys, values, table, rows, gain.reshape(1, channels)), 4 * unit,
    )
    gain_row = Held(gain_row)
    arrived = Held(arrived)
    (prefixes,) = call(
        lambda *refs: prefix_kernel(*refs, count=seq_count), "prefix",
        (near((state_rows, width)),), (arrived, order),
    )
    with jax.named_scope("scan_back"):
        entering = Held(exchange(prefixes, seq_count))
    near_queries, near_grads = Held(queries), Held(out_grad)
    attended, sums = call(
        attend_kernel, "attend",
        (near(token_shape), near((head_count, 2 * groups, width))),
        (near_queries, near_grads, gain_row, Held(inside), entering, table),
    )
    with jax.named_scope("head_sums"):
        sums = Held(lax.all_to_all(sums, "head", 0, 0, tiled=True))
    attended_grad, scales, back_pieces = call(
        lambda *refs: grad_kernel(*refs, total_channels=total_channels), "norm_grad",
        (
            Far(shape(token_shape)),
            Far(shape((width, width))),
            shape((state_rows + heads * seq_count, width)),
        ),
        (sums, Held(attended), near_grads, gain_row, near_queries, table),
        scratch=(
            pltpu.VMEM(token_shape, f32),
            pltpu.VMEM((width, width), f32),
            pltpu.SemaphoreType.DMA((heads + 1,)),
        ),
    )
    with jax.named_scope("back_out"):
        back_arrived = exchange(back_pieces, seq_count)
    output, query_grad, key_part, value_part, order = call(
        local_grad_kernel, "local_grad",
        (
            shape(token_shape, bf16),
            shape(token_shape, bf16),
            shape(token_shape),
            shape(token_shape),
            shape(tile),
        ),
        (
            attended, gain_row, scales, queries, keys, values, attended_grad, entering,
            table, rows,
        ),
        15 * unit,
    )
    suffixes, gain_sum = call(
        lambda *refs: suffix_kernel(*refs, count=seq_count), "suffix",
        (near((state_rows, width)), shape((heads, width))),
        (arrived, Held(back_arrived), order),
    )
    with jax.named_scope("back_back"):
        leaving = Held(exchange(suffixes, seq_count))
    key_grad, value_grad = call(
        finish_kernel, "finish",
        (Far(shape(token_shape, bf16)), Far(shape(token_shape, bf16))),
        (Held(keys), Held(values), leaving, table, Held(key_part), Far(value_part)),
        scratch=(
            pltpu.VMEM(token_shape, f32),
            pltpu.VMEM(token_shape, bf16),
            pltpu.VMEM(token_shape, bf16),
            pltpu.SemaphoreType.DMA((tokens // block_rows,)),
            pltpu.SemaphoreType.DMA((2 * tokens // block_rows,)),
        ),
    )
    return output, query_grad, key_grad, value_grad, gain_sum.reshape(channels)


def solution(mesh):
    in_specs = (
        P("seq", "head"),
        P("seq", "head"),
        P("seq", "head"),
        P("head", "seq"),
        P("head"),
        P("seq", "head"),
    )
    out_specs = (P("seq", "head"), P("seq", "head"), P("seq", "head"), P("seq", "head"), P("head"))
    return jax.shard_map(local, mesh=mesh, in_specs=in_specs, out_specs=out_specs, check_vma=False)
```

```python
import jax
import jax.numpy as jnp
from jax import lax
from jax.experimental import pallas as pl
from jax.experimental.pallas import tpu as pltpu
from jax.sharding import PartitionSpec as P

epsilon = 1e-06
width = 128
block_rows = 256
f32 = jnp.float32
bf16 = jnp.bfloat16


def dot(a, b, a_dim, b_dim):
    return lax.dot_general(a, b, (((a_dim,), (b_dim,)), ((), ())), preferred_element_type=f32)


def split(x):
    high = x.astype(bf16)
    return high, (x - high.astype(f32)).astype(bf16)


def side_by_side(x):
    return jnp.concatenate(split(x), axis=1)


def folded(x):
    return x[:, :width] + x[:, width:]


def dot_split_right(a, b, a_dim, b_dim):
    high, low = split(b)
    return dot(a, high, a_dim, b_dim) + dot(a, low, a_dim, b_dim)


def dot_split_left(a, b, a_dim, b_dim):
    high, low = split(a)
    return dot(high, b, a_dim, b_dim) + dot(low, b, a_dim, b_dim)


def dot_split_both(a, b, a_dim, b_dim):
    a_high, a_low = split(a)
    b_high, b_low = split(b)
    return (
        dot(a_high, b_high, a_dim, b_dim)
        + dot(a_high, b_low, a_dim, b_dim)
        + dot(a_low, b_high, a_dim, b_dim)
    )


def head_columns(ref, head):
    return ref[:, head * width : (head + 1) * width]


def block_of(array, block):
    return array[block * block_rows : (block + 1) * block_rows]


def table_column(table, kind, head, block, blocks):
    index = (3 * head + kind) * blocks + block
    return table[:, index : index + 1]


def start_column(table, head, block, blocks):
    return table_column(table, 0, head, block, blocks)


def end_column(table, head, block, blocks):
    return table_column(table, 1, head, block, blocks)


def inner_column(table, head, block, blocks):
    return table_column(table, 2, head, block, blocks)


def state_kernel(
    far_decay_ref, far_keys_ref, far_values_ref, pieces_ref, table_ref, rows_ref,
    decay_ref, keys_ref, values_ref, arrivals
):
    heads, tokens = decay_ref.shape
    decay_in = pltpu.make_async_copy(far_decay_ref, decay_ref, arrivals.at[2])
    decay_in.start()
    values_in = pltpu.make_async_copy(far_values_ref, values_ref, arrivals.at[0])
    keys_in = pltpu.make_async_copy(far_keys_ref, keys_ref, arrivals.at[1])
    values_in.start()
    keys_in.start()
    decay_in.wait()
    blocks = tokens // block_rows
    decay = decay_ref[...]
    stacked = jnp.concatenate(
        [
            decay[h : h + 1, b * block_rows : (b + 1) * block_rows]
            for h in range(heads)
            for b in range(blocks)
        ],
        axis=0,
    )
    row = lax.broadcasted_iota(jnp.int32, (block_rows, block_rows), 0)
    column = lax.broadcasted_iota(jnp.int32, (block_rows, block_rows), 1)
    upper = jnp.where(row <= column, 1.0, 0.0).astype(f32)
    sums = jnp.dot(stacked, upper, precision=lax.Precision.HIGHEST, preferred_element_type=f32)
    table_rows = []
    totals = []
    for h in range(heads):
        inside = sums[h * blocks : (h + 1) * blocks]
        offset = jnp.zeros((1, 1), f32)
        offsets = []
        for b in range(blocks):
            offsets.append(offset)
            offset = offset + inside[b : b + 1, block_rows - 1 : block_rows]
        from_device = inside + jnp.concatenate(offsets, axis=0)
        table_rows += [jnp.exp(from_device), jnp.exp(offset - from_device), inside]
        totals.append(jnp.broadcast_to(jnp.exp(offset), (1, width)))
    table_rows.append(jnp.zeros((width - 3 * blocks * heads, block_rows), f32))
    table = jnp.concatenate(table_rows, axis=0).T
    table_ref[...] = table
    rows_ref[...] = sums
    values_in.wait()
    keys_in.wait()
    for h in range(heads):
        values = head_columns(values_ref, h).astype(f32)
        weighted = jnp.concatenate(
            [
                side_by_side(end_column(table, h, b, blocks) * block_of(values, b))
                for b in range(blocks)
            ],
            axis=0,
        )
        state = folded(dot(head_columns(keys_ref, h), weighted, 0, 0))
        store_pieces(pieces_ref, h, heads, state, totals[h])


def store_pieces(pieces_ref, head, heads, state, extra):
    count = heads * width // slice_rows(pieces_ref.shape[0], heads, extra.shape[0])
    rows = heads * width // count
    stride = rows + extra.shape[0]
    per_head = count // heads
    for index in range(per_head):
        base = (head * per_head + index) * stride
        pieces_ref[base : base + rows] = state[index * rows : (index + 1) * rows]
        pieces_ref[base + rows : base + stride] = extra


def slice_rows(total, heads, extra_rows):
    return heads * width * extra_rows // (total - heads * width)


def decay_mask(table, rows, head, block, blocks, causal):
    index = head * blocks + block
    inner = inner_column(table, head, block, blocks)
    return jnp.exp(jnp.where(causal, inner - rows[index : index + 1], -1e30))


def causal_mask():
    row = lax.broadcasted_iota(jnp.int32, (block_rows, block_rows), 0)
    column = lax.broadcasted_iota(jnp.int32, (block_rows, block_rows), 1)
    return row >= column


def row_blocks(tokens):
    return [slice(b * block_rows, (b + 1) * block_rows) for b in range(tokens // block_rows)]


def stream_in(far_refs, near_refs, arrivals, order, parts):
    copies = {}
    for b in order:
        copies[b] = [
            pltpu.make_async_copy(far.at[parts[b]], near.at[parts[b]], arrivals.at[index, b])
            for index, (far, near) in enumerate(zip(far_refs, near_refs))
        ]
        for copy in copies[b]:
            copy.start()
    return copies


def stream_out(near_refs, far_refs, departures, b, part):
    copies = [
        pltpu.make_async_copy(near.at[part], far.at[part], departures.at[index, b])
        for index, (far, near) in enumerate(zip(far_refs, near_refs))
    ]
    for copy in copies:
        copy.start()
    return copies


def wait_all(copies):
    for copy in copies:
        copy.wait()


def inside_kernel(
    far_queries_ref, far_keys_ref, far_values_ref, table_ref, rows_ref, gain_in_ref,
    local_ref, gain_ref, order_ref, queries_ref, keys_ref, values_ref, arrivals
):
    tokens, channels = queries_ref.shape
    heads = channels // width
    parts = row_blocks(tokens)
    blocks = len(parts)
    arriving = stream_in(
        (far_queries_ref, far_keys_ref, far_values_ref),
        (queries_ref, keys_ref, values_ref), arrivals, range(blocks), parts,
    )
    causal = causal_mask()
    table = table_ref[...]
    rows = rows_ref[...]
    order_ref[...] = jnp.zeros(order_ref.shape, f32)
    gain_ref[...] = gain_in_ref[...]
    running = [None] * heads
    for b, part in enumerate(parts):
        wait_all(arriving[b])
        for h in range(heads):
            cut = slice(h * width, (h + 1) * width)
            query, key, value = queries_ref[part, cut], keys_ref[part, cut], values_ref[part, cut]
            mask = decay_mask(table, rows, h, b, blocks, causal)
            inner = inner_column(table, h, b, blocks)
            total = inner[block_rows - 1 : block_rows]
            scores = dot(query, key, 1, 1) * mask
            result = dot_split_left(scores, value, 1, 0)
            if b:
                carried = folded(dot(query, side_by_side(running[h]), 1, 0))
                result = result + jnp.exp(inner) * carried
            local_ref[part, cut] = result
            if b + 1 < blocks:
                weighted = jnp.exp(total - inner) * value.astype(f32)
                state = folded(dot(key, side_by_side(weighted), 0, 0))
                running[h] = state if b == 0 else jnp.exp(total) * running[h] + state


def prefix_kernel(pieces_ref, order_ref, entering_ref, *, count):
    rows = entering_ref.shape[0] // count
    stride = pieces_ref.shape[0] // count
    prefix = jnp.zeros((rows, width), f32)
    for index in range(count):
        entering_ref[index * rows : (index + 1) * rows] = prefix
        base = index * stride
        if index + 1 < count:
            prefix = (
                pieces_ref[base + rows : base + rows + 1] * prefix
                + pieces_ref[base : base + rows]
            )


def suffix_kernel(
    decay_pieces_ref, pieces_ref, order_ref, leaving_ref, gain_ref, *, count
):
    rows = leaving_ref.shape[0] // count
    stride = pieces_ref.shape[0] // count
    decay_stride = decay_pieces_ref.shape[0] // count
    suffix = jnp.zeros((rows, width), f32)
    gain_sum = jnp.zeros(gain_ref.shape, f32)
    for index in reversed(range(count)):
        leaving_ref[index * rows : (index + 1) * rows] = suffix
        base = index * stride
        decay_row = index * decay_stride + rows
        suffix = (
            decay_pieces_ref[decay_row : decay_row + 1] * suffix + pieces_ref[base : base + rows]
        )
        gain_sum = gain_sum + pieces_ref[base + rows : base + stride]
    gain_ref[...] = gain_sum


def attend_kernel(
    queries_ref, grads_ref, gain_ref, local_ref, entering_ref, table_ref, attended_ref, sums_ref
):
    tokens, channels = queries_ref.shape
    heads = channels // width
    blocks = tokens // block_rows
    groups = tokens // width
    lane = lax.broadcasted_iota(jnp.int32, (width, width), 1)
    states = [side_by_side(entering_ref[h * width : (h + 1) * width]) for h in range(heads)]
    gathered = jnp.zeros((width, width), f32)
    for b in range(blocks):
        part = slice(b * block_rows, (b + 1) * block_rows)
        squares = jnp.zeros((block_rows, width), f32)
        products = jnp.zeros((block_rows, width), f32)
        for h in range(heads):
            cut = slice(h * width, (h + 1) * width)
            carried = folded(dot(queries_ref[part, cut], states[h], 1, 0))
            attended = local_ref[part, cut] + start_column(table_ref, h, b, blocks) * carried
            attended_ref[part, cut] = attended
            squares = squares + attended * attended
            products = products + grads_ref[part, cut].astype(f32) * gain_ref[:, cut] * attended
        square_sum = jnp.sum(squares, axis=1, keepdims=True)
        product_sum = jnp.sum(products, axis=1, keepdims=True)
        for piece in range(block_rows // width):
            group = b * (block_rows // width) + piece
            inner = slice(piece * width, (piece + 1) * width)
            gathered = jnp.where(lane == group, square_sum[inner], gathered)
            gathered = jnp.where(lane == groups + group, product_sum[inner], gathered)
    compact = gathered.T[: 2 * groups]
    for index in range(sums_ref.shape[0]):
        sums_ref[index] = compact


def grad_kernel(
    sums_ref, attended_ref, grads_ref, gain_ref, queries_ref, table_ref,
    far_grad_ref, far_scales_ref, pieces_ref, attended_grad_ref, scales_ref, departures,
    *, total_channels
):
    tokens, channels = queries_ref.shape
    heads = channels // width
    blocks = tokens // block_rows
    groups = tokens // width
    sums = sums_ref[0]
    for index in range(1, sums_ref.shape[0]):
        sums = sums + sums_ref[index]
    inverse = 1.0 / jnp.sqrt(sums[:groups] / total_channels + epsilon)
    mean = inverse * sums[groups:] / total_channels
    scales = jnp.concatenate(
        [inverse, mean, jnp.zeros((width - 2 * groups, width), f32)], axis=0
    ).T
    scales_ref[...] = scales
    leaving = [pltpu.make_async_copy(scales_ref, far_scales_ref, departures.at[heads])]
    leaving[0].start()
    gain_rows = []
    backs = []
    for h in range(heads):
        cut = slice(h * width, (h + 1) * width)
        gain = gain_ref[:, cut]
        gain_sum = jnp.zeros((1, width), f32)
        weighted = []
        for group in range(groups):
            part = slice(group * width, (group + 1) * width)
            b = group * width // block_rows
            within = (group * width) % block_rows
            inverse_column = scales[:, group : group + 1]
            mean_column = scales[:, groups + group : groups + group + 1]
            grad = grads_ref[part, cut].astype(f32)
            normed = attended_ref[part, cut] * inverse_column
            gain_sum = gain_sum + jnp.sum(grad * normed, axis=0, keepdims=True)
            attended_grad = (grad * gain - normed * mean_column) * inverse_column
            attended_grad_ref[part, cut] = attended_grad
            start = start_column(table_ref[within : within + width], h, b, blocks)
            weighted.append(side_by_side(start * attended_grad))
        out = pltpu.make_async_copy(
            attended_grad_ref.at[:, cut], far_grad_ref.at[:, cut], departures.at[h]
        )
        out.start()
        leaving.append(out)
        gain_rows.append(gain_sum)
        backs.append(folded(dot(queries_ref[:, cut], jnp.concatenate(weighted, axis=0), 0, 0)))
    extra = jnp.concatenate(gain_rows, axis=0)
    for h in range(heads):
        store_pieces(pieces_ref, h, heads, backs[h], extra)
    for out in leaving:
        out.wait()


def key_value_kernel(
    far_queries_ref, far_keys_ref, far_values_ref, far_grad_ref, table_ref, rows_ref,
    far_key_part_ref, far_value_part_ref, order_ref,
    queries_ref, keys_ref, values_ref, grad_ref, key_part_ref, value_part_ref,
    arrivals, departures
):
    tokens, channels = keys_ref.shape
    heads = channels // width
    parts = row_blocks(tokens)
    blocks = len(parts)
    backward = list(reversed(range(blocks)))
    arriving = stream_in(
        (far_queries_ref, far_keys_ref, far_values_ref, far_grad_ref),
        (queries_ref, keys_ref, values_ref, grad_ref), arrivals, backward, parts,
    )
    causal = causal_mask()
    table = table_ref[...]
    rows = rows_ref[...]
    order_ref[...] = jnp.zeros(order_ref.shape, f32)
    leaving = [None] * heads
    departing = []
    for b in backward:
        part = parts[b]
        wait_all(arriving[b])
        for h in range(heads):
            cut = slice(h * width, (h + 1) * width)
            query, key, value = queries_ref[part, cut], keys_ref[part, cut], values_ref[part, cut]
            grad = grad_ref[part, cut]
            grad_high, grad_low = split(grad)
            inner = inner_column(table, h, b, blocks)
            total = inner[block_rows - 1 : block_rows]
            mask = decay_mask(table, rows, h, b, blocks, causal)
            score_grad = (dot(grad_high, value, 1, 1) + dot(grad_low, value, 1, 1)) * mask
            key_part = dot_split_left(score_grad, query, 0, 0)
            weights_high, weights_low = split(dot(query, key, 1, 1) * mask)
            value_part = (
                dot(weights_high, grad_high, 0, 0)
                + dot(weights_high, grad_low, 0, 0)
                + dot(weights_low, grad_high, 0, 0)
            )
            if b + 1 < blocks:
                to_end = jnp.exp(total - inner)
                leave_high, leave_low = split(leaving[h])
                key_part = key_part + to_end * (
                    dot(value, leave_high, 1, 1) + dot(value, leave_low, 1, 1)
                )
                value_part = value_part + to_end * (
                    dot(key, leave_high, 1, 0) + dot(key, leave_low, 1, 0)
                )
            key_part_ref[part, cut] = key_part
            value_part_ref[part, cut] = value_part
            if b:
                back = folded(dot(query, side_by_side(jnp.exp(inner) * grad), 0, 0))
                leaving[h] = back if b + 1 == blocks else back + jnp.exp(total) * leaving[h]
        departing += stream_out(
            (key_part_ref, value_part_ref), (far_key_part_ref, far_value_part_ref),
            departures, b, part,
        )
    wait_all(departing)


def query_kernel(
    far_attended_ref, far_grad_ref, far_keys_ref, far_values_ref, gain_ref, scales_ref,
    entering_ref, table_ref, rows_ref, order_ref, far_output_ref, far_query_grad_ref,
    attended_ref, grad_ref, keys_ref, values_ref, output_ref, query_grad_ref,
    arrivals, departures
):
    tokens, channels = keys_ref.shape
    heads = channels // width
    parts = row_blocks(tokens)
    blocks = len(parts)
    arriving = stream_in(
        (far_attended_ref, far_grad_ref, far_keys_ref, far_values_ref),
        (attended_ref, grad_ref, keys_ref, values_ref), arrivals, range(blocks), parts,
    )
    causal = causal_mask()
    table = table_ref[...]
    rows = rows_ref[...]
    entering = [entering_ref[h * width : (h + 1) * width] for h in range(heads)]
    departing = []
    for b, part in enumerate(parts):
        wait_all(arriving[b])
        for group in range(b * block_rows // width, (b + 1) * block_rows // width):
            piece = slice(group * width, (group + 1) * width)
            normed = attended_ref[piece] * scales_ref[:, group : group + 1]
            output_ref[piece] = (normed * gain_ref[...]).astype(bf16)
        for h in range(heads):
            cut = slice(h * width, (h + 1) * width)
            key, value = keys_ref[part, cut], values_ref[part, cut]
            grad_high, grad_low = split(grad_ref[part, cut])
            inner = inner_column(table, h, b, blocks)
            total = inner[block_rows - 1 : block_rows]
            mask = decay_mask(table, rows, h, b, blocks, causal)
            score_grad = (dot(grad_high, value, 1, 1) + dot(grad_low, value, 1, 1)) * mask
            state_high, state_low = split(entering[h])
            carried = (
                dot(grad_high, state_high, 1, 1)
                + dot(grad_high, state_low, 1, 1)
                + dot(grad_low, state_high, 1, 1)
            )
            query_grad = dot_split_left(score_grad, key, 1, 0) + jnp.exp(inner) * carried
            query_grad_ref[part, cut] = query_grad.astype(bf16)
            if b + 1 < blocks:
                weighted = jnp.exp(total - inner) * value.astype(f32)
                state = folded(dot(key, side_by_side(weighted), 0, 0))
                entering[h] = jnp.exp(total) * entering[h] + state
        departing += stream_out(
            (output_ref, query_grad_ref), (far_output_ref, far_query_grad_ref),
            departures, b, part,
        )
    wait_all(departing)


def finish_kernel(
    keys_ref, values_ref, leaving_ref, table_ref, far_key_part_ref, far_value_part_ref,
    far_key_grad_ref, far_value_grad_ref,
    key_part_ref, value_part_ref, key_grad_ref, value_grad_ref, arrivals, departures
):
    tokens, channels = keys_ref.shape
    heads = channels // width
    parts = row_blocks(tokens)
    blocks = len(parts)
    arriving = stream_in(
        (far_key_part_ref, far_value_part_ref), (key_part_ref, value_part_ref),
        arrivals, range(blocks), parts,
    )
    states = [split(leaving_ref[h * width : (h + 1) * width]) for h in range(heads)]
    departing = []
    for b, part in enumerate(parts):
        wait_all(arriving[b])
        for h in range(heads):
            cut = slice(h * width, (h + 1) * width)
            across = jnp.concatenate(states[h], axis=1)
            down = jnp.concatenate(states[h], axis=0)
            to_end = end_column(table_ref, h, b, blocks)
            key_carry = folded(dot(values_ref[part, cut], down, 1, 1))
            value_carry = folded(dot(keys_ref[part, cut], across, 1, 0))
            key_grad_ref[part, cut] = (key_part_ref[part, cut] + to_end * key_carry).astype(bf16)
            value_grad_ref[part, cut] = (
                value_part_ref[part, cut] + to_end * value_carry
            ).astype(bf16)
        departing += stream_out(
            (key_grad_ref, value_grad_ref), (far_key_grad_ref, far_value_grad_ref),
            departures, b, part,
        )
    wait_all(departing)


def shape(dims, dtype=f32):
    return jax.ShapeDtypeStruct(dims, dtype)


def near(dims, dtype=f32):
    return pltpu.VMEM(dims, dtype)


class Held:
    def __init__(self, array):
        self.array = pltpu.with_memory_space_constraint(array, pltpu.VMEM)


def exchange(pieces, count):
    flat = pieces.reshape(count, 1, pieces.shape[0] // count * width)
    return lax.all_to_all(flat, "seq", 0, 0, tiled=True).reshape(pieces.shape)


class Far:
    def __init__(self, array):
        if isinstance(array, jax.ShapeDtypeStruct):
            self.array = pltpu.HBM(array.shape, array.dtype)
        else:
            self.array = pltpu.with_memory_space_constraint(array, pltpu.HBM)


def spec_of(item):
    if isinstance(item, Far):
        return pl.BlockSpec(memory_space=pltpu.HBM)
    if isinstance(item, Held):
        return pl.BlockSpec(memory_space=pltpu.VMEM)
    return pl.BlockSpec()


def bare(item):
    return item.array if isinstance(item, (Held, Far)) else item


def call(kernel, name, out_shape, operands, flops=0, scratch=()):
    return pl.pallas_call(
        kernel,
        out_shape=tuple(bare(x) for x in out_shape),
        in_specs=[spec_of(x) for x in operands],
        out_specs=tuple(spec_of(x) for x in out_shape),
        scratch_shapes=scratch,
        compiler_params=pltpu.CompilerParams(vmem_limit_bytes=24 * 2**20),
        cost_estimate=pl.CostEstimate(flops=flops, transcendentals=0, bytes_accessed=2**20),
        name=name,
    )(*(bare(x) for x in operands))


def local(queries, keys, values, log_decay, gain, out_grad):
    tokens, channels = queries.shape
    heads = log_decay.shape[0]
    seq_count = lax.axis_size("seq")
    head_count = lax.axis_size("head")
    total_channels = float(channels * head_count)
    state_rows = heads * width
    groups = tokens // width
    tile = (8, width)
    unit = 2 * tokens * block_rows * channels
    token_shape = (tokens, channels)
    blocks = tokens // block_rows
    narrow = pltpu.VMEM(token_shape, bf16)
    wide = pltpu.VMEM(token_shape, f32)

    pieces, table, rows = call(
        state_kernel, "own_state",
        (
            shape((state_rows + seq_count, width)),
            near((block_rows, width)),
            shape((heads * tokens // block_rows, block_rows)),
        ),
        (Far(log_decay), Far(keys), Far(values)),
        scratch=(
            pltpu.VMEM(log_decay.shape, f32),
            pltpu.VMEM(token_shape, bf16),
            pltpu.VMEM(token_shape, bf16),
            pltpu.SemaphoreType.DMA((3,)),
        ),
    )
    table = Held(table)
    with jax.named_scope("scan_out"):
        arrived = exchange(pieces, seq_count)
    inside, gain_row, order = call(
        inside_kernel, "inside", (near(token_shape), near((1, channels)), shape(tile)),
        (Far(queries), Far(keys), Far(values), table, rows, gain.reshape(1, channels)), 4 * unit,
        scratch=(narrow, narrow, narrow, pltpu.SemaphoreType.DMA((3, blocks))),
    )
    gain_row = Held(gain_row)
    arrived = Held(arrived)
    (prefixes,) = call(
        lambda *refs: prefix_kernel(*refs, count=seq_count), "prefix",
        (near((state_rows, width)),), (arrived, order),
    )
    with jax.named_scope("scan_back"):
        entering = Held(exchange(prefixes, seq_count))
    near_queries, near_grads = Held(queries), Held(out_grad)
    attended, sums = call(
        attend_kernel, "attend",
        (near(token_shape), near((head_count, 2 * groups, width))),
        (near_queries, near_grads, gain_row, Held(inside), entering, table),
    )
    with jax.named_scope("head_sums"):
        sums = Held(lax.all_to_all(sums, "head", 0, 0, tiled=True))
    attended_grad, scales, back_pieces = call(
        lambda *refs: grad_kernel(*refs, total_channels=total_channels), "norm_grad",
        (
            Far(shape(token_shape)),
            Far(shape((width, width))),
            shape((state_rows + heads * seq_count, width)),
        ),
        (sums, Held(attended), near_grads, gain_row, near_queries, table),
        scratch=(
            pltpu.VMEM(token_shape, f32),
            pltpu.VMEM((width, width), f32),
            pltpu.SemaphoreType.DMA((heads + 1,)),
        ),
    )
    with jax.named_scope("back_out"):
        back_arrived = exchange(back_pieces, seq_count)
    key_part, value_part, order = call(
        key_value_kernel, "key_value",
        (Far(shape(token_shape)), Far(shape(token_shape)), shape(tile)),
        (Far(queries), Far(keys), Far(values), Far(attended_grad), table, rows), 9 * unit,
        scratch=(
            narrow, narrow, narrow, wide, wide, wide,
            pltpu.SemaphoreType.DMA((4, blocks)),
            pltpu.SemaphoreType.DMA((2, blocks)),
        ),
    )
    suffixes, gain_sum = call(
        lambda *refs: suffix_kernel(*refs, count=seq_count), "suffix",
        (shape((state_rows, width)), shape((heads, width))),
        (arrived, Held(back_arrived), order),
    )
    with jax.named_scope("back_back"):
        leaving = Held(exchange(suffixes, seq_count))
    output, query_grad = call(
        query_kernel, "query_grad",
        (Far(shape(token_shape, bf16)), Far(shape(token_shape, bf16))),
        (
            Far(attended), Far(attended_grad), Far(keys), Far(values), gain_row, scales,
            entering, table, rows, gain_sum,
        ),
        7 * unit,
        scratch=(
            wide, wide, narrow, narrow, narrow, narrow,
            pltpu.SemaphoreType.DMA((4, blocks)),
            pltpu.SemaphoreType.DMA((2, blocks)),
        ),
    )
    key_grad, value_grad = call(
        finish_kernel, "finish",
        (Far(shape(token_shape, bf16)), Far(shape(token_shape, bf16))),
        (Held(keys), Held(values), leaving, table, Far(key_part), Far(value_part)),
        scratch=(
            wide, wide, narrow, narrow,
            pltpu.SemaphoreType.DMA((2, blocks)),
            pltpu.SemaphoreType.DMA((2, blocks)),
        ),
    )
    return output, query_grad, key_grad, value_grad, gain_sum.reshape(channels)


def solution(mesh):
    in_specs = (
        P("seq", "head"),
        P("seq", "head"),
        P("seq", "head"),
        P("head", "seq"),
        P("head"),
        P("seq", "head"),
    )
    out_specs = (P("seq", "head"), P("seq", "head"), P("seq", "head"), P("seq", "head"), P("head"))
    return jax.shard_map(local, mesh=mesh, in_specs=in_specs, out_specs=out_specs, check_vma=False)
```
